512 devices in a mesh: blk: 64 (over z, y), head: 8 (over x, core).
Axes of the slice: x: 4, y: 8, z: 8, core: 2. Of those that a mesh axis runs over, the one named last changes fastest.
Arguments:
- tokens: bfloat16 [2048, 1024], P('blk'), may hold values from -6 to 6
- norm_gain: float32 [1024], replicated, may hold values from 0.25 to 1.75
- w_query: bfloat16 [1024, 1024], P(None, 'head')
- w_key: bfloat16 [1024, 1024], P(None, 'head'), may hold values from -0.1875 to 0.1875
- w_value: bfloat16 [1024, 1024], P(None, 'head'), may hold values from -0.1875 to 0.1875
- w_out: bfloat16 [1024, 1024], P('head'), may hold values from -0.1875 to 0.1875
- ffn_gain: float32 [1024], replicated, may hold values from 0.25 to 1.75
- w_gate: bfloat16 [1024, 4096], P(None, 'head'), may hold values from -0.1875 to 0.1875
- w_up: bfloat16 [1024, 4096], P(None, 'head'), may hold values from -0.1875 to 0.1875
- w_down: bfloat16 [4096, 1024], P('head'), may hold values from -0.09375 to 0.09375
- keys: bfloat16 [65536, 1024], P('blk', 'head'), may hold values from -6 to 6
- values: bfloat16 [65536, 1024], P('blk', 'head'), may hold values from -6 to 6
- key_variate: int32 [65536], P('blk'), may hold values from 0 to 3
- query_variate: int32 [2048], replicated, may hold values from 0 to 3
- bias: float32 [2, 16], P(None, 'head'), may hold values from -2 to 2
- lengths: int32 [2048], replicated, may hold values from 17 to 4096, as said below
- order: int32 [2048], replicated, may hold values from 0 to 2047, as said below
- live_blocks: int32 [1024], P('blk'), may hold values from 0 to 1
Outputs:
- layer_out: bfloat16 [2048, 1024], P('blk', 'head')
The draws below stay inside these ranges and needn't reach their ends.
Inputs may be any that keep to these rules, and one draw needn't show every extreme that they name: lengths sum to 65536; the smallest is exactly 17 and the largest exactly 4096. Each request appears once; order[j] // 32 depends only on j % 64.
All inputs are finite; a program needn't handle non-finite values.
Results may differ from the reference program's by a relative error of at most 0.025.
Values may be sent and summed in bfloat16 or wider, within the bound.
A program may use at most 64 MiB of HBM per device.

```python
import math
import jax
import jax.numpy as jnp
from jax import lax

D = 1024
H = 16
DH = 64
FF = 4096
VARIATES = 4
REQ_DEV = 32
BLOCK = 64
HD = 1024
R = 2048
POOL = 65536
NBLK = 1024
MAXLEN = 4096
MINLEN = 17


def cache_lengths(key):
    base_key = jax.random.fold_in(key, 101)
    shortest = MINLEN
    leftover = POOL - R * shortest - (MAXLEN - shortest)
    cut_points = jnp.sort(jax.random.randint(jax.random.fold_in(base_key, 1), (R - 3,), 0, leftover + 1, dtype=jnp.int32))
    boundary = jnp.concatenate([jnp.zeros((1,), jnp.int32), cut_points.astype(jnp.int32), jnp.full((1,), leftover, jnp.int32)])
    extras = boundary[1:] - boundary[:-1]
    listed = jnp.concatenate([jnp.full((1,), MAXLEN, jnp.int32), jnp.full((1,), shortest, jnp.int32), shortest + extras])
    shuffle = jax.random.permutation(jax.random.fold_in(base_key, 2), R)
    return listed[shuffle].astype(jnp.int32)


def pool_order(key):
    base_key = jax.random.fold_in(key, 202)
    groups = R // REQ_DEV
    home_list = jax.random.permutation(jax.random.fold_in(base_key, 1), groups).astype(jnp.int32)

    def pick_slots(subkey):
        return jax.random.permutation(subkey, REQ_DEV).astype(jnp.int32)
    within = jax.vmap(pick_slots)(jax.random.split(jax.random.fold_in(base_key, 2), groups))
    position = jnp.arange(R, dtype=jnp.int32)
    home_rows = home_list[position % groups]
    return (home_rows * REQ_DEV + within[home_rows, position // groups]).astype(jnp.int32)


def chosen_requests(key):
    return jax.random.permutation(jax.random.fold_in(key, 303), R)[:4].astype(jnp.int32)


def sign_pattern(key, salt, count):
    return (2 * jax.random.randint(jax.random.fold_in(key, salt), (count,), 0, 2, dtype=jnp.int32) - 1).astype(jnp.float32)


def drawn_rows(key):
    lengths_drawn = cache_lengths(key)
    order_drawn = pool_order(key)
    ends = jnp.cumsum(lengths_drawn[order_drawn]).astype(jnp.int32)
    position = jnp.arange(POOL, dtype=jnp.int32)
    rank = jnp.searchsorted(ends, position, side='right').astype(jnp.int32)
    owner = order_drawn[rank]
    offset = position - (ends[rank] - lengths_drawn[owner])
    match = owner[:, None] == chosen_requests(key)[None, :]
    planted = jnp.any(match, axis=1) & (offset < 8)
    return (match, planted, offset)


def draw_lengths(key, part):
    return cache_lengths(key)


def draw_order(key, part):
    return pool_order(key)


def draw_live_blocks(key, part):
    match, planted, offset = drawn_rows(key)
    coins = jax.random.randint(jax.random.fold_in(key, 808), (NBLK,), 0, 4, dtype=jnp.int32)
    base_live = (coins > 0).astype(jnp.int32)
    position = jnp.arange(POOL, dtype=jnp.int32)
    forced = jnp.zeros((NBLK,), jnp.int32).at[position // BLOCK].max(planted.astype(jnp.int32))
    return jnp.maximum(base_live, forced).astype(jnp.int32)


def draw_tokens(key, part):
    pattern = sign_pattern(key, 606, D)
    column = jnp.arange(D, dtype=jnp.float32) / jnp.float32(D - 1)
    base = jnp.clip(jax.random.normal(jax.random.fold_in(key, 909), (R, D), jnp.float32), -6.0, 6.0)
    ramp = 0.2 + 0.8 * column
    request_ids = jnp.arange(R, dtype=jnp.int32)
    picked = jnp.any(request_ids[:, None] == chosen_requests(key)[None, :], axis=1)
    return jnp.where(picked[:, None], 6.0 * pattern[None, :], base * ramp[None, :]).astype(jnp.bfloat16)


def draw_w_query(key, part):
    token_pattern = sign_pattern(key, 606, D)
    key_pattern = sign_pattern(key, 404, HD)
    base = jnp.clip(jax.random.normal(jax.random.fold_in(key, 707), (D, HD), jnp.float32), -6.0, 6.0) / math.sqrt(D)
    return (base + 6.0 / D * token_pattern[:, None] * key_pattern[None, :]).astype(jnp.bfloat16)


def draw_keys(key, part):
    match, planted, offset = drawn_rows(key)
    pattern = sign_pattern(key, 404, HD)
    noise = jnp.clip(jax.random.normal(jax.random.fold_in(key, 505), (POOL, HD), jnp.float32), -6.0, 6.0)
    strengths = jnp.array([4.5, 3.5, 2.5, 1.5], jnp.float32)
    strength = jnp.sum(jnp.where(match, strengths[None, :], jnp.float32(0.0)), axis=1)
    level = strength - offset.astype(jnp.float32) * (2.0 / (6.0 * math.sqrt(DH)))
    return jnp.where(planted[:, None], level[:, None] * pattern[None, :], noise).astype(jnp.bfloat16)


def place_ends(values, own_key, low, largest):
    place = [jax.random.randint(jax.random.fold_in(own_key, axis), (), 0, length) for axis, length in enumerate(values.shape)]
    main_axis = values.shape.index(max(values.shape))
    beside = place[:main_axis] + [(place[main_axis] + 1) % values.shape[main_axis]] + place[main_axis + 1:]
    return values.at[tuple(place)].set(low).at[tuple(beside)].set(largest)


def steps_of(rng, shape, cuts, low, largest):
    factor_of = 1.0
    for axis_at, blocks in cuts:
        heights = jax.random.uniform(jax.random.fold_in(jax.random.fold_in(rng, 6), axis_at), (blocks,), jnp.float32, low / len(cuts), largest / len(cuts))
        factor_of = factor_of * jnp.repeat(jnp.exp(heights), shape[axis_at] // blocks).reshape((-1,) + (1,) * (len(shape) - 1 - axis_at))
    return factor_of


def normal_values(key, extent, spread, most, shards=(), held_as=jnp.bfloat16):
    level = steps_of(key, extent, shards, -0.22, 0.18) if shards else 1.0
    result = jax.random.normal(key, extent, jnp.float32) * spread * level
    return jnp.minimum(jnp.maximum(result, -most), most).astype(held_as)


def setup_inputs(seed: int = 0) -> dict:
    key_list = jax.random.split(jax.random.key(seed), 19)
    return {
        "tokens": draw_tokens(jax.random.fold_in(key_list[18], 71), 0),
        "norm_gain": jnp.clip(1.0 + 0.15 * jax.random.normal(key_list[1], (D,), jnp.float32), 0.25, 1.75),
        "w_query": draw_w_query(jax.random.fold_in(key_list[18], 71), 0),
        "w_key": normal_values(key_list[3], (D, HD), D ** -0.5, 0.1875, ((1, 8),)),
        "w_value": normal_values(key_list[4], (D, HD), D ** -0.5, 0.1875, ((1, 8),)),
        "w_out": normal_values(key_list[5], (HD, D), HD ** -0.5, 0.1875, ((0, 8),)),
        "ffn_gain": jnp.clip(1.0 + 0.15 * jax.random.normal(key_list[6], (D,), jnp.float32), 0.25, 1.75),
        "w_gate": normal_values(key_list[7], (D, FF), D ** -0.5, 0.1875, ((1, 8),)),
        "w_up": normal_values(key_list[8], (D, FF), D ** -0.5, 0.1875, ((1, 8),)),
        "w_down": normal_values(key_list[9], (FF, D), FF ** -0.5, 0.09375, ((0, 8),)),
        "keys": draw_keys(jax.random.fold_in(key_list[18], 71), 0),
        "values": normal_values(key_list[11], (POOL, HD), 1.0, 6.0, ((0, 64), (1, 8))),
        "key_variate": place_ends(jax.random.randint(key_list[12], (POOL,), 0, VARIATES), jax.random.fold_in(key_list[12], 1), 0, VARIATES - 1).astype(jnp.int32),
        "query_variate": place_ends(jax.random.randint(key_list[13], (R,), 0, VARIATES), jax.random.fold_in(key_list[13], 1), 0, VARIATES - 1).astype(jnp.int32),
        "bias": jnp.clip(jax.random.uniform(key_list[14], (2, H), jnp.float32, -2.0, 2.0) * steps_of(key_list[14], (2, H), ((1, 8),), -0.4, 0.0), -2.0, 2.0),
        "lengths": draw_lengths(jax.random.fold_in(key_list[18], 71), 0),
        "order": draw_order(jax.random.fold_in(key_list[18], 71), 0),
        "live_blocks": draw_live_blocks(jax.random.fold_in(key_list[18], 71), 0),
    }


def normalize(inputs, gain):
    mean_square = lax.optimization_barrier(jnp.mean(inputs * inputs, axis=-1, keepdims=True))
    return inputs * lax.rsqrt(mean_square + 1e-05) * gain

def reference(tokens, norm_gain, w_query, w_key, w_value, w_out, ffn_gain, w_gate, w_up, w_down, keys, values, key_variate, query_variate, bias, lengths, order, live_blocks):
    inputs = tokens.astype(jnp.float32)
    normed = normalize(inputs, norm_gain).astype(jnp.bfloat16)
    query = jnp.dot(normed, w_query, preferred_element_type=jnp.float32).astype(jnp.bfloat16)
    key_new = jnp.dot(normed, w_key, preferred_element_type=jnp.float32).astype(jnp.bfloat16)
    value_new = jnp.dot(normed, w_value, preferred_element_type=jnp.float32).astype(jnp.bfloat16)
    ends = jnp.cumsum(lengths[order]).astype(jnp.int32)
    position = jnp.arange(POOL, dtype=jnp.int32)
    rank = jnp.searchsorted(ends, position, side='right').astype(jnp.int32)
    owner = order[rank]
    live = jnp.repeat(live_blocks, POOL // live_blocks.shape[0]) > 0
    query_heads = query.astype(jnp.float32).reshape(R, H, DH)
    key_heads = keys.astype(jnp.float32).reshape(POOL, H, DH)
    raw = lax.optimization_barrier(jnp.sum(query_heads[owner] * key_heads, axis=2)) / jnp.sqrt(jnp.float32(DH))
    same = key_variate == query_variate[owner]
    score = raw + jnp.where(same[:, None], bias[0][None, :], bias[1][None, :])
    own = lax.optimization_barrier(jnp.sum(query_heads * key_new.astype(jnp.float32).reshape(R, H, DH), axis=2)) / jnp.sqrt(jnp.float32(DH)) + bias[0][None, :]
    masked = jnp.where(live[:, None], score, jnp.float32(-1e+30))
    top = jnp.full((R, H), -1e+30, jnp.float32).at[owner].max(masked)
    top = jnp.maximum(top, own)
    weight = jnp.where(live[:, None], jnp.exp(masked - top[owner]), jnp.float32(0.0))
    own_weight = jnp.exp(own - top)
    total = jax.ops.segment_sum(weight, owner, num_segments=R) + own_weight
    value_heads = values.astype(jnp.float32).reshape(POOL, H, DH)
    summed = jax.ops.segment_sum(weight[:, :, None] * value_heads, owner, num_segments=R)
    summed = summed + own_weight[:, :, None] * value_new.astype(jnp.float32).reshape(R, H, DH)
    attended = (summed / total[:, :, None]).reshape(R, H * DH).astype(jnp.bfloat16)
    mixed = (inputs + jnp.dot(attended, w_out, preferred_element_type=jnp.float32)).astype(jnp.bfloat16)
    hidden_in = normalize(mixed.astype(jnp.float32), ffn_gain).astype(jnp.bfloat16)
    gate = jnp.dot(hidden_in, w_gate, preferred_element_type=jnp.float32)
    upper = jnp.dot(hidden_in, w_up, preferred_element_type=jnp.float32)
    hidden = (jax.nn.silu(gate) * upper).astype(jnp.bfloat16)
    return (mixed.astype(jnp.float32) + jnp.dot(hidden, w_down, preferred_element_type=jnp.float32)).astype(jnp.bfloat16)
```

```python
import functools

import jax
import jax.numpy as jnp
from jax import lax
from jax.experimental import pallas as pl
from jax.experimental.pallas import tpu as pltpu
from jax.sharding import PartitionSpec as P

F32 = jnp.float32
BF16 = jnp.bfloat16
HIGH = lax.Precision.HIGHEST
FLOOR = -1e30


def iota(shape, dim):
    return lax.broadcasted_iota(jnp.int32, shape, dim)


def dot(a, b):
    return jnp.dot(a, b, preferred_element_type=F32)


def dot_nt(a, b, precision=None):
    return lax.dot_general(
        a, b, (((1,), (1,)), ((), ())), preferred_element_type=F32, precision=precision
    )


def dot_tn(a, b, precision=None):
    return lax.dot_general(
        a, b, (((0,), (0,)), ((), ())), preferred_element_type=F32, precision=precision
    )


def row_dot(a, b):
    return jnp.dot(a, b, preferred_element_type=F32, precision=HIGH)


def kernel(
    tok_ref,
    norm_gain_ref,
    ffn_gain_ref,
    order_ref,
    len_ref,
    query_variate_ref,
    key_variate_ref,
    live_ref,
    bias_ref,
    wq_hbm,
    wk_hbm,
    wv_hbm,
    keys_hbm,
    values_hbm,
    wo_hbm,
    wg_hbm,
    wu_hbm,
    wd_hbm,
    out_ref,
    wq,
    wk,
    wv,
    keys,
    values,
    wo,
    wg,
    wu,
    wd,
    q_send,
    q_recv,
    p_send,
    p_recv,
    c_send,
    c_recv,
    d_recv,
    e_send,
    e_recv,
    load_sem,
    send_sem,
    recv_sem,
):
    n_blk = q_send.shape[0]
    n_head = c_send.shape[0]
    reqs, d_model = tok_ref.shape
    pool = keys.shape[0]
    n_live = live_ref.shape[1]
    block = pool // n_live
    width = c_send.shape[2]
    half = width // 2
    me = lax.axis_index("blk")
    head = lax.axis_index("head")

    loads = []
    for at, (src, dst) in enumerate(
        (
            (wq_hbm, wq),
            (wk_hbm, wk),
            (wv_hbm, wv),
            (keys_hbm, keys),
            (values_hbm, values),
            (wo_hbm, wo),
            (wg_hbm, wg),
            (wu_hbm, wu),
            (wd_hbm, wd),
        )
    ):
        copy = pltpu.make_async_copy(src, dst, load_sem.at[at])
        copy.start()
        loads.append(copy)

    barrier = pltpu.get_barrier_semaphore()

    def greet_blk(i, carry):
        pl.semaphore_signal(barrier, inc=1, device_id={"blk": lax.rem(me + i, n_blk)})
        return carry

    def greet_head(i, carry):
        pl.semaphore_signal(barrier, inc=1, device_id={"head": lax.rem(head + i, n_head)})
        return carry

    lax.fori_loop(1, n_blk, greet_blk, 0)
    lax.fori_loop(1, n_head, greet_head, 0)

    order = order_ref[...]
    rows, lanes = order.shape
    home = order[0:1, :] >> 5
    local = order & (reqs - 1)
    packed = (len_ref[...] + (query_variate_ref[...] << 13)).astype(F32)
    per_row = lanes // reqs
    table = jnp.zeros((reqs, lanes), F32)
    for part in range(per_row):
        pick = (home == iota((rows, lanes), 0) * per_row + part).astype(F32)
        found = dot_tn(packed, pick, HIGH)
        table = table + found[part * reqs : (part + 1) * reqs, :]
    ordered = jnp.zeros((rows, lanes), F32)
    for slot in range(reqs):
        ordered = ordered + jnp.where(local == slot, table[slot : slot + 1, :], 0.0)
    ordered = ordered.astype(jnp.int32)
    variate = (ordered >> 13).astype(F32)
    length = (ordered & 8191).astype(F32)
    upper = (iota((lanes, lanes), 0) <= iota((lanes, lanes), 1)).astype(F32)
    prefix = row_dot(length, upper)
    below = (iota((rows, rows), 1) < iota((rows, rows), 0)).astype(F32)
    totals = jnp.broadcast_to(jnp.sum(length, axis=1, keepdims=True), (rows, lanes))
    ends = prefix + row_dot(below, totals)
    starts = ends - length

    mine = jnp.where(home == me, local, -1)
    start_acc = jnp.zeros((reqs, lanes), F32)
    end_acc = jnp.zeros((reqs, lanes), F32)
    slot_id = iota((reqs, lanes), 0)
    for row in range(rows):
        hit = mine[row : row + 1, :] == slot_id
        start_acc = start_acc + jnp.where(hit, starts[row : row + 1, :], 0.0)
        end_acc = end_acc + jnp.where(hit, ends[row : row + 1, :], 0.0)
    start_req = jnp.sum(start_acc, axis=1, keepdims=True)
    end_req = jnp.sum(end_acc, axis=1, keepdims=True)
    first = (iota((reqs, n_blk), 1) * pool).astype(F32)
    holds = (end_req > first) & (start_req < first + pool)
    holds_f = holds.astype(F32)

    inputs = tok_ref[...].astype(F32)
    mean_square = jnp.mean(inputs * inputs, axis=1, keepdims=True)
    normed = (inputs * lax.rsqrt(mean_square + 1e-05) * norm_gain_ref[...]).astype(BF16)
    loads[0].wait()
    query = dot(normed, wq[...]).astype(BF16)
    query_f = query.astype(F32)
    routed = dot_tn(holds_f.astype(BF16), query)
    q_send[...] = routed.reshape(n_blk, 1, width)
    q_recv[pl.ds(me, 1)] = q_send[pl.ds(me, 1)]

    pl.semaphore_wait(barrier, n_blk + n_head - 2)

    def exchange_blk(send, recv, at):
        def step(i, carry):
            to = lax.rem(me + i, n_blk)
            pltpu.make_async_remote_copy(
                src_ref=send.at[to],
                dst_ref=recv.at[me],
                send_sem=send_sem.at[at],
                recv_sem=recv_sem.at[at],
                device_id={"blk": to},
            ).start()
            return carry

        lax.fori_loop(1, n_blk, step, 0)

    def exchange_head(send, recv, at):
        def step(i, carry):
            to = lax.rem(head + i, n_head)
            pltpu.make_async_remote_copy(
                src_ref=send(to),
                dst_ref=recv.at[head],
                send_sem=send_sem.at[at],
                recv_sem=recv_sem.at[at],
                device_id={"head": to},
            ).start()
            return carry

        lax.fori_loop(1, n_head, step, 0)

    def wait_bytes(ref, sem, at):
        part = ref.at[pl.ds(0, ref.shape[0] - 1)]
        pltpu.make_async_copy(part, part, sem.at[at]).wait()

    exchange_blk(q_send, q_recv, 0)

    loads[1].wait()
    key_new = dot(normed, wk[...]).astype(BF16).astype(F32)
    loads[2].wait()
    value_new = dot(normed, wv[...]).astype(BF16).astype(F32)
    product = query_f * key_new
    left = iota((reqs, width), 1) < half
    scale = 1.0 / (half**0.5)
    own = [
        jnp.sum(jnp.where(left, product, 0.0), axis=1, keepdims=True) * scale + bias_ref[0, 0],
        jnp.sum(jnp.where(left, 0.0, product), axis=1, keepdims=True) * scale + bias_ref[0, 1],
    ]
    base = (me * pool).astype(F32)
    meets = (ends > base) & (starts < base + pool)
    start_lane = jnp.sum(jnp.where(meets, starts - base, 0.0), axis=0, keepdims=True)
    end_lane = jnp.sum(jnp.where(meets, ends - base, 0.0), axis=0, keepdims=True)
    variate_lane = jnp.sum(jnp.where(meets, variate, 0.0), axis=0, keepdims=True)
    at_home = home == iota((n_blk, lanes), 0)
    start_slot = jnp.sum(jnp.where(at_home, start_lane, 0.0), axis=1, keepdims=True)
    end_slot = jnp.sum(jnp.where(at_home, end_lane, 0.0), axis=1, keepdims=True)
    variate_slot = jnp.sum(jnp.where(at_home, variate_lane, 0.0), axis=1, keepdims=True)
    in_block = (iota((n_live, pool), 1) // block == iota((n_live, pool), 0)).astype(BF16)
    live = dot(jnp.broadcast_to(live_ref[...].astype(F32).astype(BF16), (8, n_live)), in_block)[0:1, :]
    token = iota((n_blk, pool), 1).astype(F32)
    mask = (token >= start_slot) & (token < end_slot) & (live > 0.5)
    same = key_variate_ref[...].astype(F32) == variate_slot
    loads[3].wait()
    loads[4].wait()

    wait_bytes(q_recv, recv_sem, 0)
    queries = q_recv[...].reshape(n_blk, width)
    left_slot = iota((n_blk, width), 1) < half
    stacked = jnp.concatenate(
        [jnp.where(left_slot, queries, 0.0), jnp.where(left_slot, 0.0, queries)], axis=0
    ).astype(BF16)
    raw = dot_nt(stacked, keys[...])
    tops, sums, weights = [], [], []
    for at in range(2):
        score = raw[at * n_blk : (at + 1) * n_blk, :] * scale + jnp.where(
            same, bias_ref[0, at], bias_ref[1, at]
        )
        top = jnp.max(jnp.where(mask, score, FLOOR), axis=1, keepdims=True)
        weight = jnp.where(mask, jnp.exp(score - top), 0.0)
        tops.append(top)
        sums.append(jnp.sum(weight, axis=1, keepdims=True))
        weights.append(weight.astype(BF16))
    summed = dot(jnp.concatenate(weights, axis=0), values[...])
    summed = jnp.where(left_slot, summed[:n_blk, :], summed[n_blk:, :])
    column = iota((n_blk, width), 1)
    stats = jnp.where(
        column < 1,
        tops[0],
        jnp.where(column < 2, tops[1], jnp.where(column < 3, sums[0], sums[1])),
    )
    p_send[:, 0:1, :] = summed.reshape(n_blk, 1, width)
    p_send[:, 1:2, :] = stats.reshape(n_blk, 1, width)
    p_recv[pl.ds(me, 1)] = p_send[pl.ds(me, 1)]
    exchange_blk(p_send, p_recv, 1)
    wait_bytes(p_recv, recv_sem, 1)

    part_sum = p_recv[:, 0:1, :].reshape(n_blk, width)
    part_stat = p_recv[:, 1:2, :].reshape(n_blk, width)
    choose = (iota((8, width), 0) == iota((8, width), 1)).astype(F32)
    by_lane = dot_nt(choose, part_stat, HIGH)
    merged, total = [], []
    own_weight = []
    for at in range(2):
        part_top = by_lane[at : at + 1, :]
        part_total = by_lane[2 + at : 3 + at, :]
        top = jnp.maximum(
            own[at], jnp.max(jnp.where(holds, part_top, FLOOR), axis=1, keepdims=True)
        )
        factor = jnp.where(holds, jnp.exp(part_top - top), 0.0)
        mine_weight = jnp.exp(own[at] - top)
        total.append(jnp.sum(factor * part_total, axis=1, keepdims=True) + mine_weight)
        own_weight.append(mine_weight)
        merged.append(row_dot(factor, part_sum))
    value_final = jnp.where(left, merged[0], merged[1]) + jnp.where(
        left, own_weight[0], own_weight[1]
    ) * value_new
    attended = (value_final / jnp.where(left, total[0], total[1])).astype(BF16)
    loads[5].wait()
    projected = dot(attended, wo[...]).astype(BF16)
    for at in range(n_head):
        c_send[at] = projected[:, at * width : (at + 1) * width]
    c_recv[pl.ds(head, 1)] = c_send[pl.ds(head, 1)]
    exchange_head(lambda to: c_send.at[to], c_recv, 2)
    wait_bytes(c_recv, recv_sem, 2)
    mixed = tok_ref[:, pl.ds(pl.multiple_of(head * width, width), width)].astype(F32)
    part = c_recv[0].astype(F32)
    for at in range(1, n_head):
        part = part + c_recv[at].astype(F32)
    mixed = (mixed + part).astype(BF16)
    d_recv[pl.ds(head, 1)] = mixed.reshape(1, reqs, width)
    exchange_head(lambda to: d_recv.at[head], d_recv, 3)
    wait_bytes(d_recv, recv_sem, 3)
    square = jnp.zeros((reqs, width), F32)
    gathered = []
    for at in range(n_head):
        piece = d_recv[at].astype(F32)
        gathered.append(piece)
        square = square + piece * piece
    inverse = lax.rsqrt(jnp.sum(square, axis=1, keepdims=True) / d_model + 1e-05)
    hidden_in = jnp.concatenate(
        [
            (gathered[at] * inverse * ffn_gain_ref[:, at * width : (at + 1) * width]).astype(BF16)
            for at in range(n_head)
        ],
        axis=1,
    )
    loads[6].wait()
    gate = dot(hidden_in, wg[...])
    loads[7].wait()
    upper_units = dot(hidden_in, wu[...])
    hidden = (gate * jax.nn.sigmoid(gate) * upper_units).astype(BF16)
    loads[8].wait()
    down = dot(hidden, wd[...]).astype(BF16)
    for at in range(n_head):
        e_send[at] = down[:, at * width : (at + 1) * width]
    e_recv[pl.ds(head, 1)] = e_send[pl.ds(head, 1)]
    exchange_head(lambda to: e_send.at[to], e_recv, 4)
    wait_bytes(e_recv, recv_sem, 4)
    part = e_recv[0].astype(F32)
    for at in range(1, n_head):
        part = part + e_recv[at].astype(F32)
    out_ref[...] = (mixed.astype(F32) + part).astype(BF16)
    wait_bytes(q_send, send_sem, 0)
    wait_bytes(p_send, send_sem, 1)
    wait_bytes(c_send, send_sem, 2)
    wait_bytes(d_recv, send_sem, 3)
    wait_bytes(e_send, send_sem, 4)


def body(
    tokens,
    norm_gain,
    w_query,
    w_key,
    w_value,
    w_out,
    ffn_gain,
    w_gate,
    w_up,
    w_down,
    keys,
    values,
    key_variate,
    query_variate,
    bias,
    lengths,
    order,
    live_blocks,
):
    n_blk = lax.axis_size("blk")
    n_head = lax.axis_size("head")
    reqs, d_model = tokens.shape
    width = d_model // n_head
    vmem = pl.BlockSpec(memory_space=pltpu.VMEM)
    smem = pl.BlockSpec(memory_space=pltpu.SMEM)
    hbm = pl.BlockSpec(memory_space=pl.ANY)
    big = (w_query, w_key, w_value, keys, values, w_out, w_gate, w_up, w_down)
    return pl.pallas_call(
        kernel,
        out_shape=jax.ShapeDtypeStruct((reqs, width), BF16),
        in_specs=[vmem] * 8 + [smem] + [hbm] * len(big),
        out_specs=vmem,
        scratch_shapes=[pltpu.VMEM(x.shape, x.dtype) for x in big]
        + [
            pltpu.VMEM((n_blk, 1, width), F32),
            pltpu.VMEM((n_blk, 1, width), F32),
            pltpu.VMEM((n_blk, 2, width), F32),
            pltpu.VMEM((n_blk, 2, width), F32),
        ]
        + [pltpu.VMEM((n_head, reqs, width), BF16)] * 5
        + [
            pltpu.SemaphoreType.DMA((len(big),)),
            pltpu.SemaphoreType.DMA((5,)),
            pltpu.SemaphoreType.DMA((5,)),
        ],
        compiler_params=pltpu.CompilerParams(
            collective_id=0, has_side_effects=True, vmem_limit_bytes=40 * 1024 * 1024
        ),
    )(
        tokens,
        norm_gain.reshape(1, -1),
        ffn_gain.reshape(1, -1),
        order.reshape(-1, 128),
        lengths.reshape(-1, 128),
        query_variate.reshape(-1, 128),
        key_variate.reshape(1, -1),
        live_blocks.reshape(1, -1),
        bias,
        *big,
    )


def solution(mesh):
    placed = (
        P("blk", None),
        P(),
        P(None, "head"),
        P(None, "head"),
        P(None, "head"),
        P("head", None),
        P(),
        P(None, "head"),
        P(None, "head"),
        P("head", None),
        P("blk", "head"),
        P("blk", "head"),
        P("blk"),
        P(),
        P(None, "head"),
        P(),
        P(),
        P("blk"),
    )
    return jax.shard_map(
        body, mesh=mesh, in_specs=placed, out_specs=P("blk", "head"), check_vma=False
    )
```

```python
import jax
import jax.numpy as jnp
from jax import lax
from jax.experimental import pallas as pl
from jax.experimental.pallas import tpu as pltpu
from jax.sharding import PartitionSpec as P

F32 = jnp.float32
BF16 = jnp.bfloat16
HIGH = lax.Precision.HIGHEST
FLOOR = -1e30


def iota(shape, dim):
    return lax.broadcasted_iota(jnp.int32, shape, dim)


def dot(a, b):
    return jnp.dot(a, b, preferred_element_type=F32)


def dot_nt(a, b, precision=None):
    return lax.dot_general(
        a, b, (((1,), (1,)), ((), ())), preferred_element_type=F32, precision=precision
    )


def dot_tn(a, b, precision=None):
    return lax.dot_general(
        a, b, (((0,), (0,)), ((), ())), preferred_element_type=F32, precision=precision
    )


def row_dot(a, b):
    return jnp.dot(a, b, preferred_element_type=F32, precision=HIGH)


LOADS = (
    "order",
    "lens",
    "query_variate",
    "tok",
    "norm_gain",
    "wq",
    "wk",
    "wv",
    "key_variate",
    "live",
    "keys",
    "values",
    "wo",
    "ffn_gain",
    "wg",
    "wu",
    "wd",
)


def kernel(*refs):
    n_loads = len(LOADS)
    bias_ref = refs[0]
    from_hbm = dict(zip(LOADS, refs[1 : 1 + n_loads]))
    out_ref = refs[1 + n_loads]
    at_vmem = dict(zip(LOADS, refs[2 + n_loads : 2 + 2 * n_loads]))
    (
        q_send,
        q_recv,
        p_send,
        p_recv,
        c_send,
        c_recv,
        d_recv,
        e_send,
        e_recv,
        load_sem,
        send_sem,
        recv_sem,
    ) = refs[2 + 2 * n_loads :]
    n_blk = q_send.shape[0]
    n_head = c_send.shape[0]
    reqs, d_model = at_vmem["tok"].shape
    pool = at_vmem["keys"].shape[0]
    n_live = at_vmem["live"].shape[1]
    block = pool // n_live
    width = c_send.shape[2]
    half = width // 2
    me = lax.axis_index("blk")
    head = lax.axis_index("head")

    copies = {
        name: pltpu.make_async_copy(from_hbm[name], at_vmem[name], load_sem.at[at])
        for at, name in enumerate(LOADS)
    }
    loaded = set()
    sent = []

    def need(name):
        if name not in loaded:
            loaded.add(name)
            copies[name].wait()
        return at_vmem[name]

    barrier = pltpu.get_barrier_semaphore()

    def greet_blk(i, carry):
        pl.semaphore_signal(barrier, inc=1, device_id={"blk": lax.rem(me + i, n_blk)})
        return carry

    def greet_head(i, carry):
        pl.semaphore_signal(barrier, inc=1, device_id={"head": lax.rem(head + i, n_head)})
        return carry

    lax.fori_loop(1, n_blk, greet_blk, 0)
    lax.fori_loop(1, n_head, greet_head, 0)
    for name in LOADS:
        copies[name].start()

    order = need("order")[...]
    rows, lanes = order.shape
    home = order[0:1, :] >> 5
    local = order & (reqs - 1)
    packed = (need("lens")[...] + (need("query_variate")[...] << 13)).astype(F32)
    per_row = lanes // reqs
    table = jnp.zeros((reqs, lanes), F32)
    for part in range(per_row):
        pick = (home == iota((rows, lanes), 0) * per_row + part).astype(F32)
        found = dot_tn(packed, pick, HIGH)
        table = table + found[part * reqs : (part + 1) * reqs, :]
    ordered = jnp.zeros((rows, lanes), F32)
    for slot in range(reqs):
        ordered = ordered + jnp.where(local == slot, table[slot : slot + 1, :], 0.0)
    ordered = ordered.astype(jnp.int32)
    variate = (ordered >> 13).astype(F32)
    length = (ordered & 8191).astype(F32)
    upper = (iota((lanes, lanes), 0) <= iota((lanes, lanes), 1)).astype(F32)
    prefix = row_dot(length, upper)
    below = (iota((rows, rows), 1) < iota((rows, rows), 0)).astype(F32)
    totals = jnp.broadcast_to(jnp.sum(length, axis=1, keepdims=True), (rows, lanes))
    ends = prefix + row_dot(below, totals)
    starts = ends - length

    mine = jnp.where(home == me, local, -1)
    start_acc = jnp.zeros((reqs, lanes), F32)
    end_acc = jnp.zeros((reqs, lanes), F32)
    slot_id = iota((reqs, lanes), 0)
    for row in range(rows):
        hit = mine[row : row + 1, :] == slot_id
        start_acc = start_acc + jnp.where(hit, starts[row : row + 1, :], 0.0)
        end_acc = end_acc + jnp.where(hit, ends[row : row + 1, :], 0.0)
    start_req = jnp.sum(start_acc, axis=1, keepdims=True)
    end_req = jnp.sum(end_acc, axis=1, keepdims=True)
    first = (iota((reqs, n_blk), 1) * pool).astype(F32)
    holds = (end_req > first) & (start_req < first + pool)
    holds_f = holds.astype(F32)

    inputs = need("tok")[...].astype(F32)
    mean_square = jnp.mean(inputs * inputs, axis=1, keepdims=True)
    normed = (inputs * lax.rsqrt(mean_square + 1e-05) * need("norm_gain")[...]).astype(BF16)
    query = dot(normed, need("wq")[...]).astype(BF16)
    query_f = query.astype(F32)
    routed = dot_tn(holds_f.astype(BF16), query)
    q_send[...] = routed.reshape(n_blk, 1, width)
    q_recv[pl.ds(me, 1)] = q_send[pl.ds(me, 1)]

    pl.semaphore_wait(barrier, n_blk + n_head - 2)

    def exchange_blk(send, recv, at):
        def step(i, carry):
            to = lax.rem(me + i, n_blk)
            pltpu.make_async_remote_copy(
                src_ref=send.at[to],
                dst_ref=recv.at[me],
                send_sem=send_sem.at[at],
                recv_sem=recv_sem.at[at],
                device_id={"blk": to},
            ).start()
            return carry

        lax.fori_loop(1, n_blk, step, 0)
        sent.append((send, at))

    def exchange_head(send, recv, at):
        def step(i, carry):
            to = lax.rem(head + i, n_head)
            pltpu.make_async_remote_copy(
                src_ref=send(to),
                dst_ref=recv.at[head],
                send_sem=send_sem.at[at],
                recv_sem=recv_sem.at[at],
                device_id={"head": to},
            ).start()
            return carry

        lax.fori_loop(1, n_head, step, 0)
        sent.append((recv, at))

    def wait_bytes(ref, sem, at):
        part = ref.at[pl.ds(0, ref.shape[0] - 1)]
        pltpu.make_async_copy(part, part, sem.at[at]).wait()

    exchange_blk(q_send, q_recv, 0)

    key_new = dot(normed, need("wk")[...]).astype(BF16).astype(F32)
    value_new = dot(normed, need("wv")[...]).astype(BF16).astype(F32)
    product = query_f * key_new
    left = iota((reqs, width), 1) < half
    scale = 1.0 / (half**0.5)
    own = [
        jnp.sum(jnp.where(left, product, 0.0), axis=1, keepdims=True) * scale + bias_ref[0, 0],
        jnp.sum(jnp.where(left, 0.0, product), axis=1, keepdims=True) * scale + bias_ref[0, 1],
    ]
    base = (me * pool).astype(F32)
    meets = (ends > base) & (starts < base + pool)
    start_lane = jnp.sum(jnp.where(meets, starts - base, 0.0), axis=0, keepdims=True)
    end_lane = jnp.sum(jnp.where(meets, ends - base, 0.0), axis=0, keepdims=True)
    variate_lane = jnp.sum(jnp.where(meets, variate, 0.0), axis=0, keepdims=True)
    at_home = home == iota((n_blk, lanes), 0)
    start_slot = jnp.sum(jnp.where(at_home, start_lane, 0.0), axis=1, keepdims=True)
    end_slot = jnp.sum(jnp.where(at_home, end_lane, 0.0), axis=1, keepdims=True)
    variate_slot = jnp.sum(jnp.where(at_home, variate_lane, 0.0), axis=1, keepdims=True)
    in_block = (iota((n_live, pool), 1) // block == iota((n_live, pool), 0)).astype(BF16)
    live = dot(jnp.broadcast_to(need("live")[...].astype(F32).astype(BF16), (8, n_live)), in_block)[0:1, :]
    token = iota((n_blk, pool), 1).astype(F32)
    mask = (token >= start_slot) & (token < end_slot) & (live > 0.5)
    same = need("key_variate")[...].astype(F32) == variate_slot

    wait_bytes(q_recv, recv_sem, 0)
    queries = q_recv[...].reshape(n_blk, width)
    left_slot = iota((n_blk, width), 1) < half
    stacked = jnp.concatenate(
        [jnp.where(left_slot, queries, 0.0), jnp.where(left_slot, 0.0, queries)], axis=0
    ).astype(BF16)
    raw = dot_nt(stacked, need("keys")[...])
    tops, sums, weights = [], [], []
    for at in range(2):
        score = raw[at * n_blk : (at + 1) * n_blk, :] * scale + jnp.where(
            same, bias_ref[0, at], bias_ref[1, at]
        )
        top = jnp.max(jnp.where(mask, score, FLOOR), axis=1, keepdims=True)
        weight = jnp.where(mask, jnp.exp(score - top), 0.0)
        tops.append(top)
        sums.append(jnp.sum(weight, axis=1, keepdims=True))
        weights.append(weight.astype(BF16))
    summed = dot(jnp.concatenate(weights, axis=0), need("values")[...])
    summed = jnp.where(left_slot, summed[:n_blk, :], summed[n_blk:, :])
    column = iota((n_blk, width), 1)
    stats = jnp.where(
        column < 1,
        tops[0],
        jnp.where(column < 2, tops[1], jnp.where(column < 3, sums[0], sums[1])),
    )
    p_send[:, 0:1, :] = summed.reshape(n_blk, 1, width)
    p_send[:, 1:2, :] = stats.reshape(n_blk, 1, width)
    p_recv[pl.ds(me, 1)] = p_send[pl.ds(me, 1)]
    exchange_blk(p_send, p_recv, 1)
    wait_bytes(p_recv, recv_sem, 1)

    part_sum = p_recv[:, 0:1, :].reshape(n_blk, width)
    part_stat = p_recv[:, 1:2, :].reshape(n_blk, width)
    choose = (iota((8, width), 0) == iota((8, width), 1)).astype(F32)
    by_lane = dot_nt(choose, part_stat, HIGH)
    merged, total = [], []
    own_weight = []
    for at in range(2):
        part_top = by_lane[at : at + 1, :]
        part_total = by_lane[2 + at : 3 + at, :]
        top = jnp.maximum(
            own[at], jnp.max(jnp.where(holds, part_top, FLOOR), axis=1, keepdims=True)
        )
        factor = jnp.where(holds, jnp.exp(part_top - top), 0.0)
        mine_weight = jnp.exp(own[at] - top)
        total.append(jnp.sum(factor * part_total, axis=1, keepdims=True) + mine_weight)
        own_weight.append(mine_weight)
        merged.append(row_dot(factor, part_sum))
    value_final = jnp.where(left, merged[0], merged[1]) + jnp.where(
        left, own_weight[0], own_weight[1]
    ) * value_new
    attended = (value_final / jnp.where(left, total[0], total[1])).astype(BF16)
    projected = dot(attended, need("wo")[...]).astype(BF16)
    for at in range(n_head):
        c_send[at] = projected[:, at * width : (at + 1) * width]
    c_recv[pl.ds(head, 1)] = c_send[pl.ds(head, 1)]
    exchange_head(lambda to: c_send.at[to], c_recv, 2)
    wait_bytes(c_recv, recv_sem, 2)
    mixed = need("tok")[:, pl.ds(pl.multiple_of(head * width, width), width)].astype(F32)
    part = c_recv[0].astype(F32)
    for at in range(1, n_head):
        part = part + c_recv[at].astype(F32)
    mixed = (mixed + part).astype(BF16)
    d_recv[pl.ds(head, 1)] = mixed.reshape(1, reqs, width)
    exchange_head(lambda to: d_recv.at[head], d_recv, 3)
    wait_bytes(d_recv, recv_sem, 3)
    square = jnp.zeros((reqs, width), F32)
    gathered = []
    for at in range(n_head):
        piece = d_recv[at].astype(F32)
        gathered.append(piece)
        square = square + piece * piece
    inverse = lax.rsqrt(jnp.sum(square, axis=1, keepdims=True) / d_model + 1e-05)
    hidden_in = jnp.concatenate(
        [
            (gathered[at] * inverse * need("ffn_gain")[:, at * width : (at + 1) * width]).astype(BF16)
            for at in range(n_head)
        ],
        axis=1,
    )
    gate = dot(hidden_in, need("wg")[...])
    upper_units = dot(hidden_in, need("wu")[...])
    hidden = (gate * jax.nn.sigmoid(gate) * upper_units).astype(BF16)
    down = dot(hidden, need("wd")[...]).astype(BF16)
    for at in range(n_head):
        e_send[at] = down[:, at * width : (at + 1) * width]
    e_recv[pl.ds(head, 1)] = e_send[pl.ds(head, 1)]
    exchange_head(lambda to: e_send.at[to], e_recv, 4)
    wait_bytes(e_recv, recv_sem, 4)
    part = e_recv[0].astype(F32)
    for at in range(1, n_head):
        part = part + e_recv[at].astype(F32)
    out_ref[...] = (mixed.astype(F32) + part).astype(BF16)
    for ref, at in sent:
        wait_bytes(ref, send_sem, at)


def body(
    tokens,
    norm_gain,
    w_query,
    w_key,
    w_value,
    w_out,
    ffn_gain,
    w_gate,
    w_up,
    w_down,
    keys,
    values,
    key_variate,
    query_variate,
    bias,
    lengths,
    order,
    live_blocks,
):
    n_blk = lax.axis_size("blk")
    n_head = lax.axis_size("head")
    reqs, d_model = tokens.shape
    width = d_model // n_head
    operands = dict(
        tok=tokens,
        norm_gain=norm_gain.reshape(1, -1),
        ffn_gain=ffn_gain.reshape(1, -1),
        order=order.reshape(-1, 128),
        lens=lengths.reshape(-1, 128),
        query_variate=query_variate.reshape(-1, 128),
        key_variate=key_variate.reshape(1, -1),
        live=live_blocks.reshape(1, -1),
        wq=w_query,
        wk=w_key,
        wv=w_value,
        keys=keys,
        values=values,
        wo=w_out,
        wg=w_gate,
        wu=w_up,
        wd=w_down,
    )
    loads = [operands[name] for name in LOADS]
    return pl.pallas_call(
        kernel,
        out_shape=jax.ShapeDtypeStruct((reqs, width), BF16),
        in_specs=[pl.BlockSpec(memory_space=pltpu.SMEM)]
        + [pl.BlockSpec(memory_space=pltpu.HBM)] * len(loads),
        out_specs=pl.BlockSpec(memory_space=pltpu.VMEM),
        scratch_shapes=[pltpu.VMEM(x.shape, x.dtype) for x in loads]
        + [
            pltpu.VMEM((n_blk, 1, width), F32),
            pltpu.VMEM((n_blk, 1, width), F32),
            pltpu.VMEM((n_blk, 2, width), F32),
            pltpu.VMEM((n_blk, 2, width), F32),
        ]
        + [pltpu.VMEM((n_head, reqs, width), BF16)] * 5
        + [
            pltpu.SemaphoreType.DMA((len(loads),)),
            pltpu.SemaphoreType.DMA((5,)),
            pltpu.SemaphoreType.DMA((5,)),
        ],
        compiler_params=pltpu.CompilerParams(
            collective_id=0, has_side_effects=True, vmem_limit_bytes=56 * 1024 * 1024
        ),
    )(bias, *loads)


def solution(mesh):
    placed = (
        P("blk", None),
        P(),
        P(None, "head"),
        P(None, "head"),
        P(None, "head"),
        P("head", None),
        P(),
        P(None, "head"),
        P(None, "head"),
        P("head", None),
        P("blk", "head"),
        P("blk", "head"),
        P("blk"),
        P(),
        P(None, "head"),
        P(),
        P(),
        P("blk"),
    )
    return jax.shard_map(
        body, mesh=mesh, in_specs=placed, out_specs=P("blk", "head"), check_vma=False
    )
```

```python
import jax
import jax.numpy as jnp
from jax import lax
from jax.experimental import pallas as pl
from jax.experimental.pallas import tpu as pltpu
from jax.sharding import PartitionSpec as P

F32 = jnp.float32
BF16 = jnp.bfloat16
HIGH = lax.Precision.HIGHEST
FLOOR = -1e30
SIDE = 8


def iota(shape, dim):
    return lax.broadcasted_iota(jnp.int32, shape, dim)


def dot(a, b):
    return jnp.dot(a, b, preferred_element_type=F32)


def dot_nt(a, b, precision=None):
    return lax.dot_general(
        a, b, (((1,), (1,)), ((), ())), preferred_element_type=F32, precision=precision
    )


def dot_tn(a, b, precision=None):
    return lax.dot_general(
        a, b, (((0,), (0,)), ((), ())), preferred_element_type=F32, precision=precision
    )


def row_dot(a, b):
    return jnp.dot(a, b, preferred_element_type=F32, precision=HIGH)


LOADS = (
    "order",
    "lens",
    "query_variate",
    "tok",
    "norm_gain",
    "wq",
    "wk",
    "wv",
    "key_variate",
    "live",
    "keys",
    "values",
    "wo",
    "ffn_gain",
    "wg",
    "wu",
    "wd",
)


def fold(k):
    return SIDE // 2 + ((k + 1) // 2) * (1 - 2 * lax.rem(k, 2))


def each_blk(me, act):
    z, y = me // SIDE, lax.rem(me, SIDE)
    for both in range(2 * SIDE - 2):

        def step(a, carry):
            to_z = lax.rem(z + fold(a), SIDE)
            to_y = lax.rem(y + fold(both - a), SIDE)
            act(to_z * SIDE + to_y)
            return carry

        lax.fori_loop(max(0, both - SIDE + 1), min(both, SIDE - 1) + 1, step, 0)


def each_head(head, n_head, act):
    chip, core = head // 2, lax.rem(head, 2)
    chips = n_head // 2
    for far in (2, 1, 3):
        to = lax.rem(chip + far, chips) * 2
        act(to + core)
        act(to + 1 - core)
    act(chip * 2 + 1 - core)


def kernel(*refs):
    n_loads = len(LOADS)
    bias_ref = refs[0]
    from_hbm = dict(zip(LOADS, refs[1 : 1 + n_loads]))
    out_ref = refs[1 + n_loads]
    at_vmem = dict(zip(LOADS, refs[2 + n_loads : 2 + 2 * n_loads]))
    (
        q_send,
        q_recv,
        p_send,
        p_recv,
        c_recv,
        e_send,
        e_recv,
        mixed_ref,
        load_sem,
        send_sem,
        recv_sem,
    ) = refs[2 + 2 * n_loads :]
    n_blk = q_send.shape[0]
    n_head = c_recv.shape[0]
    reqs, d_model = at_vmem["tok"].shape
    pool = at_vmem["keys"].shape[0]
    n_live = at_vmem["live"].shape[1]
    block = pool // n_live
    width = c_recv.shape[2]
    half = width // 2
    me = lax.axis_index("blk")
    head = lax.axis_index("head")

    wo_all = at_vmem["wo"]
    at_vmem["wo"] = wo_all.at[head]
    copies = {
        name: pltpu.make_async_copy(from_hbm[name], at_vmem[name], load_sem.at[at])
        for at, name in enumerate(LOADS)
    }
    loaded = set()
    sent = []

    def need(name):
        if name not in loaded:
            loaded.add(name)
            copies[name].wait()
        return at_vmem[name]

    barrier = pltpu.get_barrier_semaphore()

    each_blk(me, lambda to: pl.semaphore_signal(barrier, inc=1, device_id={"blk": to}))
    each_head(
        head, n_head, lambda to: pl.semaphore_signal(barrier, inc=1, device_id={"head": to})
    )
    for name in LOADS:
        copies[name].start()

    order = need("order")[...]
    rows, lanes = order.shape
    home = order[0:1, :] >> 5
    local = order & (reqs - 1)
    packed = (need("lens")[...] + (need("query_variate")[...] << 13)).astype(F32)
    per_row = lanes // reqs
    table = jnp.zeros((reqs, lanes), F32)
    for part in range(per_row):
        pick = (home == iota((rows, lanes), 0) * per_row + part).astype(F32)
        found = dot_tn(packed, pick, HIGH)
        table = table + found[part * reqs : (part + 1) * reqs, :]
    ordered = jnp.zeros((rows, lanes), F32)
    for slot in range(reqs):
        ordered = ordered + jnp.where(local == slot, table[slot : slot + 1, :], 0.0)
    ordered = ordered.astype(jnp.int32)
    variate = (ordered >> 13).astype(F32)
    length = (ordered & 8191).astype(F32)
    upper = (iota((lanes, lanes), 0) <= iota((lanes, lanes), 1)).astype(F32)
    prefix = row_dot(length, upper)
    below = (iota((rows, rows), 1) < iota((rows, rows), 0)).astype(F32)
    totals = jnp.broadcast_to(jnp.sum(length, axis=1, keepdims=True), (rows, lanes))
    ends = prefix + row_dot(below, totals)
    starts = ends - length

    mine = jnp.where(home == me, local, -1)
    start_acc = jnp.zeros((reqs, lanes), F32)
    end_acc = jnp.zeros((reqs, lanes), F32)
    slot_id = iota((reqs, lanes), 0)
    for row in range(rows):
        hit = mine[row : row + 1, :] == slot_id
        start_acc = start_acc + jnp.where(hit, starts[row : row + 1, :], 0.0)
        end_acc = end_acc + jnp.where(hit, ends[row : row + 1, :], 0.0)
    start_req = jnp.sum(start_acc, axis=1, keepdims=True)
    end_req = jnp.sum(end_acc, axis=1, keepdims=True)
    first = (iota((reqs, n_blk), 1) * pool).astype(F32)
    holds = (end_req > first) & (start_req < first + pool)
    holds_f = holds.astype(F32)

    inputs = need("tok")[...].astype(F32)
    mean_square = jnp.mean(inputs * inputs, axis=1, keepdims=True)
    normed = (inputs * lax.rsqrt(mean_square + 1e-05) * need("norm_gain")[...]).astype(BF16)
    query = dot(normed, need("wq")[...]).astype(BF16)
    query_f = query.astype(F32)
    routed = dot_tn(holds_f.astype(BF16), query)
    q_send[...] = routed.reshape(n_blk, 1, width)
    q_recv[pl.ds(me, 1)] = q_send[pl.ds(me, 1)]

    pl.semaphore_wait(barrier, n_blk + n_head - 2)

    def exchange_blk(send, recv, at):
        def start(to):
            pltpu.make_async_remote_copy(
                src_ref=send.at[to],
                dst_ref=recv.at[me],
                send_sem=send_sem.at[at],
                recv_sem=recv_sem.at[at],
                device_id={"blk": to},
            ).start()

        each_blk(me, start)
        sent.append((send, n_blk - 1, at))

    def exchange_head(send, recv, at):
        def start(to):
            pltpu.make_async_remote_copy(
                src_ref=send(to),
                dst_ref=recv.at[head],
                send_sem=send_sem.at[at],
                recv_sem=recv_sem.at[at],
                device_id={"head": to},
            ).start()

        each_head(head, n_head, start)
        sent.append((recv, n_head - 1, at))

    def share(src, slot, to, at):
        pltpu.make_async_remote_copy(
            src_ref=src,
            dst_ref=wo_all.at[slot],
            send_sem=send_sem.at[at],
            recv_sem=recv_sem.at[at],
            device_id={"head": to},
        ).start()

    def wait_bytes(ref, count, sem, at):
        part = ref.at[pl.ds(0, count)]
        pltpu.make_async_copy(part, part, sem.at[at]).wait()

    exchange_blk(q_send, q_recv, 0)

    chips = n_head // 2
    sibling = (head // 2) * 2 + 1 - lax.rem(head, 2)
    for far in (2, 1, 3):
        share(from_hbm["wo"], head, lax.rem(head + 2 * far, n_head), 4)
    share(from_hbm["wo"], head, sibling, 5)
    sent.append((wo_all, chips - 1, 4))
    sent.append((wo_all, chips, 5))

    key_new = dot(normed, need("wk")[...]).astype(BF16).astype(F32)
    value_new = dot(normed, need("wv")[...]).astype(BF16).astype(F32)
    product = query_f * key_new
    left = iota((reqs, width), 1) < half
    scale = 1.0 / (half**0.5)
    own = [
        jnp.sum(jnp.where(left, product, 0.0), axis=1, keepdims=True) * scale + bias_ref[0, 0],
        jnp.sum(jnp.where(left, 0.0, product), axis=1, keepdims=True) * scale + bias_ref[0, 1],
    ]
    base = (me * pool).astype(F32)
    meets = (ends > base) & (starts < base + pool)
    start_lane = jnp.sum(jnp.where(meets, starts - base, 0.0), axis=0, keepdims=True)
    end_lane = jnp.sum(jnp.where(meets, ends - base, 0.0), axis=0, keepdims=True)
    variate_lane = jnp.sum(jnp.where(meets, variate, 0.0), axis=0, keepdims=True)
    at_home = home == iota((n_blk, lanes), 0)
    start_slot = jnp.sum(jnp.where(at_home, start_lane, 0.0), axis=1, keepdims=True)
    end_slot = jnp.sum(jnp.where(at_home, end_lane, 0.0), axis=1, keepdims=True)
    variate_slot = jnp.sum(jnp.where(at_home, variate_lane, 0.0), axis=1, keepdims=True)
    in_block = (iota((n_live, pool), 1) // block == iota((n_live, pool), 0)).astype(BF16)
    live = dot(jnp.broadcast_to(need("live")[...].astype(F32).astype(BF16), (8, n_live)), in_block)[0:1, :]
    token = iota((n_blk, pool), 1).astype(F32)
    mask = (token >= start_slot) & (token < end_slot) & (live > 0.5)
    same = need("key_variate")[...].astype(F32) == variate_slot

    wait_bytes(q_recv, n_blk - 1, recv_sem, 0)
    queries = q_recv[...].reshape(n_blk, width)
    left_slot = iota((n_blk, width), 1) < half
    stacked = jnp.concatenate(
        [jnp.where(left_slot, queries, 0.0), jnp.where(left_slot, 0.0, queries)], axis=0
    ).astype(BF16)
    raw = dot_nt(stacked, need("keys")[...])
    tops, sums, weights = [], [], []
    for at in range(2):
        score = raw[at * n_blk : (at + 1) * n_blk, :] * scale + jnp.where(
            same, bias_ref[0, at], bias_ref[1, at]
        )
        top = jnp.max(jnp.where(mask, score, FLOOR), axis=1, keepdims=True)
        weight = jnp.where(mask, jnp.exp(score - top), 0.0)
        tops.append(top)
        sums.append(jnp.sum(weight, axis=1, keepdims=True))
        weights.append(weight.astype(BF16))
    summed = dot(jnp.concatenate(weights, axis=0), need("values")[...])
    summed = jnp.where(left_slot, summed[:n_blk, :], summed[n_blk:, :])
    column = iota((n_blk, width), 1)
    stats = jnp.where(
        column < 1,
        tops[0],
        jnp.where(column < 2, tops[1], jnp.where(column < 3, sums[0], sums[1])),
    )
    p_send[:, 0:1, :] = summed.reshape(n_blk, 1, width)
    p_send[:, 1:2, :] = stats.reshape(n_blk, 1, width)
    p_recv[pl.ds(me, 1)] = p_send[pl.ds(me, 1)]
    exchange_blk(p_send, p_recv, 1)
    wait_bytes(wo_all, chips - 1, recv_sem, 4)
    for far in (2, 1, 3):
        slot = lax.rem(head + 2 * far, n_head)
        share(wo_all.at[slot], slot, sibling, 5)
    wait_bytes(p_recv, n_blk - 1, recv_sem, 1)

    part_sum = p_recv[:, 0:1, :].reshape(n_blk, width)
    part_stat = p_recv[:, 1:2, :].reshape(n_blk, width)
    choose = (iota((8, width), 0) == iota((8, width), 1)).astype(F32)
    by_lane = dot_nt(choose, part_stat, HIGH)
    merged, total = [], []
    own_weight = []
    for at in range(2):
        part_top = by_lane[at : at + 1, :]
        part_total = by_lane[2 + at : 3 + at, :]
        top = jnp.maximum(
            own[at], jnp.max(jnp.where(holds, part_top, FLOOR), axis=1, keepdims=True)
        )
        factor = jnp.where(holds, jnp.exp(part_top - top), 0.0)
        mine_weight = jnp.exp(own[at] - top)
        total.append(jnp.sum(factor * part_total, axis=1, keepdims=True) + mine_weight)
        own_weight.append(mine_weight)
        merged.append(row_dot(factor, part_sum))
    value_final = jnp.where(left, merged[0], merged[1]) + jnp.where(
        left, own_weight[0], own_weight[1]
    ) * value_new
    attended = (value_final / jnp.where(left, total[0], total[1])).astype(BF16)
    c_recv[pl.ds(head, 1)] = attended.reshape(1, reqs, width)
    exchange_head(lambda to: c_recv.at[head], c_recv, 2)
    wait_bytes(wo_all, chips, recv_sem, 5)
    need("wo")
    wait_bytes(c_recv, n_head - 1, recv_sem, 2)
    attended_all = jnp.concatenate([c_recv[at] for at in range(n_head)], axis=1)
    projected = dot(attended_all, wo_all[...].reshape(d_model, d_model))
    mixed = (inputs + projected).astype(BF16).astype(F32)
    for at in range(n_head):
        mixed_ref[at] = mixed[:, at * width : (at + 1) * width]
    inverse = lax.rsqrt(jnp.mean(mixed * mixed, axis=1, keepdims=True) + 1e-05)
    hidden_in = (mixed * inverse * need("ffn_gain")[...]).astype(BF16)
    gate = dot(hidden_in, need("wg")[...])
    upper_units = dot(hidden_in, need("wu")[...])
    hidden = (gate * jax.nn.sigmoid(gate) * upper_units).astype(BF16)
    down = dot(hidden, need("wd")[...]).astype(BF16)
    for at in range(n_head):
        e_send[at] = down[:, at * width : (at + 1) * width]
    e_recv[pl.ds(head, 1)] = e_send[pl.ds(head, 1)]
    exchange_head(lambda to: e_send.at[to], e_recv, 3)
    wait_bytes(e_recv, n_head - 1, recv_sem, 3)
    part = e_recv[0].astype(F32)
    for at in range(1, n_head):
        part = part + e_recv[at].astype(F32)
    out_ref[...] = (mixed_ref[head] + part).astype(BF16)
    for ref, count, at in sent:
        wait_bytes(ref, count, send_sem, at)


def body(
    tokens,
    norm_gain,
    w_query,
    w_key,
    w_value,
    w_out,
    ffn_gain,
    w_gate,
    w_up,
    w_down,
    keys,
    values,
    key_variate,
    query_variate,
    bias,
    lengths,
    order,
    live_blocks,
):
    n_blk = lax.axis_size("blk")
    n_head = lax.axis_size("head")
    reqs, d_model = tokens.shape
    width = d_model // n_head
    operands = dict(
        tok=tokens,
        norm_gain=norm_gain.reshape(1, -1),
        ffn_gain=ffn_gain.reshape(1, -1),
        order=order.reshape(-1, 128),
        lens=lengths.reshape(-1, 128),
        query_variate=query_variate.reshape(-1, 128),
        key_variate=key_variate.reshape(1, -1),
        live=live_blocks.reshape(1, -1),
        wq=w_query,
        wk=w_key,
        wv=w_value,
        keys=keys,
        values=values,
        wo=w_out,
        wg=w_gate,
        wu=w_up,
        wd=w_down,
    )
    loads = [operands[name] for name in LOADS]
    return pl.pallas_call(
        kernel,
        out_shape=jax.ShapeDtypeStruct((reqs, width), BF16),
        in_specs=[pl.BlockSpec(memory_space=pltpu.SMEM)]
        + [pl.BlockSpec(memory_space=pltpu.HBM)] * len(loads),
        out_specs=pl.BlockSpec(memory_space=pltpu.VMEM),
        scratch_shapes=[
            pltpu.VMEM((n_head,) * (name == "wo") + x.shape, x.dtype)
            for name, x in zip(LOADS, loads)
        ]
        + [
            pltpu.VMEM((n_blk, 1, width), F32),
            pltpu.VMEM((n_blk, 1, width), F32),
            pltpu.VMEM((n_blk, 2, width), F32),
            pltpu.VMEM((n_blk, 2, width), F32),
        ]
        + [pltpu.VMEM((n_head, reqs, width), BF16)] * 3
        + [pltpu.VMEM((n_head, reqs, width), F32)]
        + [
            pltpu.SemaphoreType.DMA((len(loads),)),
            pltpu.SemaphoreType.DMA((6,)),
            pltpu.SemaphoreType.DMA((6,)),
        ],
        compiler_params=pltpu.CompilerParams(
            collective_id=0, has_side_effects=True, vmem_limit_bytes=56 * 1024 * 1024
        ),
    )(bias, *loads)


def solution(mesh):
    placed = (
        P("blk", None),
        P(),
        P(None, "head"),
        P(None, "head"),
        P(None, "head"),
        P("head", None),
        P(),
        P(None, "head"),
        P(None, "head"),
        P("head", None),
        P("blk", "head"),
        P("blk", "head"),
        P("blk"),
        P(),
        P(None, "head"),
        P(),
        P(),
        P("blk"),
    )
    return jax.shard_map(
        body, mesh=mesh, in_specs=placed, out_specs=P("blk", "head"), check_vma=False
    )
```

```python
import jax
import jax.numpy as jnp
from jax import lax
from jax.experimental import pallas as pl
from jax.experimental.pallas import tpu as pltpu
from jax.sharding import PartitionSpec as P

F32 = jnp.float32
BF16 = jnp.bfloat16
HIGH = lax.Precision.HIGHEST
FLOOR = -1e30
SIDE = 8
EARLY = 6


def iota(shape, dim):
    return lax.broadcasted_iota(jnp.int32, shape, dim)


def dot(a, b):
    return jnp.dot(a, b, preferred_element_type=F32)


def dot_nt(a, b, precision=None):
    return lax.dot_general(
        a, b, (((1,), (1,)), ((), ())), preferred_element_type=F32, precision=precision
    )


def dot_tn(a, b, precision=None):
    return lax.dot_general(
        a, b, (((0,), (0,)), ((), ())), preferred_element_type=F32, precision=precision
    )


def row_dot(a, b):
    return jnp.dot(a, b, preferred_element_type=F32, precision=HIGH)


LOADS = (
    "order",
    "lens",
    "query_variate",
    "tok",
    "norm_gain",
    "wq",
    "wk",
    "wv",
    "key_variate",
    "live",
    "keys",
    "values",
    "wo",
    "ffn_gain",
    "wg",
    "wu",
    "wd",
)


def ring(k):
    return min(k, SIDE - k)


FAR_FIRST = sorted(
    ((dz, dy) for dz in range(SIDE) for dy in range(SIDE) if dz or dy),
    key=lambda step: -ring(step[0]) - ring(step[1]),
)


def each_blk(me, act):
    low = SIDE - 1
    for dz, dy in FAR_FIRST:
        act(((me + SIDE * dz) & (SIDE * low)) | ((me + dy) & low))


def each_head(head, n_head, act):
    for far in (2, 1, 3):
        to = (head + 2 * far) & (n_head - 1)
        act(to)
        act(to ^ 1)
    act(head ^ 1)


def kernel(*refs):
    n_loads = len(LOADS)
    bias_ref = refs[0]
    from_hbm = dict(zip(LOADS, refs[1 : 1 + n_loads]))
    out_ref = refs[1 + n_loads]
    at_vmem = dict(zip(LOADS, refs[2 + n_loads : 2 + 2 * n_loads]))
    (
        q_send,
        q_recv,
        p_send,
        p_recv,
        c_recv,
        e_send,
        e_recv,
        mixed_ref,
        load_sem,
        send_sem,
        recv_sem,
    ) = refs[2 + 2 * n_loads :]
    n_blk = q_send.shape[0]
    n_head = c_recv.shape[0]
    reqs, d_model = at_vmem["tok"].shape
    pool = at_vmem["keys"].shape[0]
    n_live = at_vmem["live"].shape[1]
    block = pool // n_live
    width = c_recv.shape[2]
    half = width // 2
    scale = 1.0 / (half**0.5)
    me = lax.axis_index("blk")
    head = lax.axis_index("head")

    wo_all = at_vmem["wo"]
    at_vmem["wo"] = wo_all.at[head]
    copies = {
        name: pltpu.make_async_copy(from_hbm[name], at_vmem[name], load_sem.at[at])
        for at, name in enumerate(LOADS)
    }
    loaded = set()
    sent = []

    def need(name):
        if name not in loaded:
            loaded.add(name)
            copies[name].wait()
        return at_vmem[name]

    barrier = pltpu.get_barrier_semaphore()

    for name in LOADS[:EARLY]:
        copies[name].start()
    each_blk(me, lambda to: pl.semaphore_signal(barrier, inc=1, device_id={"blk": to}))
    each_head(
        head, n_head, lambda to: pl.semaphore_signal(barrier, inc=1, device_id={"head": to})
    )
    for name in LOADS[EARLY:]:
        copies[name].start()

    order = need("order")[...]
    rows, lanes = order.shape
    home = order[0:1, :] >> 5
    local = order & (reqs - 1)
    packed = (need("lens")[...] + (need("query_variate")[...] << 13)).astype(F32)
    per_row = lanes // reqs
    table = jnp.zeros((reqs, lanes), F32)
    for part in range(per_row):
        pick = (home == iota((rows, lanes), 0) * per_row + part).astype(F32)
        found = dot_tn(packed, pick, HIGH)
        table = table + found[part * reqs : (part + 1) * reqs, :]
    ordered = jnp.zeros((rows, lanes), F32)
    for slot in range(reqs):
        ordered = ordered + jnp.where(local == slot, table[slot : slot + 1, :], 0.0)
    ordered = ordered.astype(jnp.int32)
    variate = (ordered >> 13).astype(F32)
    length = (ordered & 8191).astype(F32)
    upper = (iota((lanes, lanes), 0) <= iota((lanes, lanes), 1)).astype(F32)
    prefix = row_dot(length, upper)
    below = (iota((rows, rows), 1) < iota((rows, rows), 0)).astype(F32)
    totals = jnp.broadcast_to(jnp.sum(length, axis=1, keepdims=True), (rows, lanes))
    ends = prefix + row_dot(below, totals)
    starts = ends - length

    mine = jnp.where(home == me, local, -1)
    start_acc = jnp.zeros((reqs, lanes), F32)
    end_acc = jnp.zeros((reqs, lanes), F32)
    slot_id = iota((reqs, lanes), 0)
    for row in range(rows):
        hit = mine[row : row + 1, :] == slot_id
        start_acc = start_acc + jnp.where(hit, starts[row : row + 1, :], 0.0)
        end_acc = end_acc + jnp.where(hit, ends[row : row + 1, :], 0.0)
    start_req = jnp.sum(start_acc, axis=1, keepdims=True)
    end_req = jnp.sum(end_acc, axis=1, keepdims=True)
    first = (iota((reqs, n_blk), 1) * pool).astype(F32)
    holds = (end_req > first) & (start_req < first + pool)
    holds_f = holds.astype(F32)

    inputs = need("tok")[...].astype(F32)
    mean_square = jnp.mean(inputs * inputs, axis=1, keepdims=True)
    normed = (inputs * lax.rsqrt(mean_square + 1e-05) * need("norm_gain")[...]).astype(BF16)
    query = dot(normed, need("wq")[...]).astype(BF16)
    query_f = query.astype(F32)
    routed = dot_tn(holds_f.astype(BF16), query) * scale
    q_send[...] = routed.reshape(n_blk, 1, width)
    q_recv[pl.ds(me, 1)] = q_send[pl.ds(me, 1)]

    pl.semaphore_wait(barrier, n_blk + n_head - 2)

    def exchange_blk(send, recv, at):
        def start(to):
            pltpu.make_async_remote_copy(
                src_ref=send.at[to],
                dst_ref=recv.at[me],
                send_sem=send_sem.at[at],
                recv_sem=recv_sem.at[at],
                device_id={"blk": to},
            ).start()

        each_blk(me, start)
        sent.append((send, n_blk - 1, at))

    def exchange_head(send, recv, at):
        def start(to):
            pltpu.make_async_remote_copy(
                src_ref=send(to),
                dst_ref=recv.at[head],
                send_sem=send_sem.at[at],
                recv_sem=recv_sem.at[at],
                device_id={"head": to},
            ).start()

        each_head(head, n_head, start)
        sent.append((recv, n_head - 1, at))

    def share(src, slot, to, at):
        pltpu.make_async_remote_copy(
            src_ref=src,
            dst_ref=wo_all.at[slot],
            send_sem=send_sem.at[at],
            recv_sem=recv_sem.at[at],
            device_id={"head": to},
        ).start()

    def wait_bytes(ref, count, sem, at):
        part = ref.at[pl.ds(0, count)]
        pltpu.make_async_copy(part, part, sem.at[at]).wait()

    exchange_blk(q_send, q_recv, 0)

    chips = n_head // 2
    sibling = head ^ 1
    for far in (2, 1, 3):
        share(from_hbm["wo"], head, (head + 2 * far) & (n_head - 1), 4)
    share(from_hbm["wo"], head, sibling, 5)
    sent.append((wo_all, chips - 1, 4))
    sent.append((wo_all, chips, 5))

    key_new = dot(normed, need("wk")[...]).astype(BF16).astype(F32)
    value_new = dot(normed, need("wv")[...]).astype(BF16).astype(F32)
    product = query_f * key_new
    left = iota((reqs, width), 1) < half
    own = [
        jnp.sum(jnp.where(left, product, 0.0), axis=1, keepdims=True) * scale + bias_ref[0, 0],
        jnp.sum(jnp.where(left, 0.0, product), axis=1, keepdims=True) * scale + bias_ref[0, 1],
    ]
    base = (me * pool).astype(F32)
    meets = (ends > base) & (starts < base + pool)
    start_lane = jnp.sum(jnp.where(meets, starts - base, 0.0), axis=0, keepdims=True)
    end_lane = jnp.sum(jnp.where(meets, ends - base, 0.0), axis=0, keepdims=True)
    variate_lane = jnp.sum(jnp.where(meets, variate, 0.0), axis=0, keepdims=True)
    at_home = home == iota((n_blk, lanes), 0)
    start_slot = jnp.sum(jnp.where(at_home, start_lane, 0.0), axis=1, keepdims=True)
    end_slot = jnp.sum(jnp.where(at_home, end_lane, 0.0), axis=1, keepdims=True)
    variate_slot = jnp.sum(jnp.where(at_home, variate_lane, 0.0), axis=1, keepdims=True)
    in_block = (iota((n_live, pool), 1) // block == iota((n_live, pool), 0)).astype(BF16)
    live = dot(jnp.broadcast_to(need("live")[...].astype(F32).astype(BF16), (8, n_live)), in_block)[0:1, :]
    token = iota((n_blk, pool), 1).astype(F32)
    mask = (token >= start_slot) & (token < end_slot) & (live > 0.5)
    same = need("key_variate")[...].astype(F32) == variate_slot

    shift = [
        jnp.where(mask, jnp.where(same, bias_ref[0, at], bias_ref[1, at]), FLOOR)
        for at in range(2)
    ]
    wait_bytes(q_recv, n_blk - 1, recv_sem, 0)
    queries = q_recv[...].reshape(n_blk, width)
    left_slot = iota((n_blk, width), 1) < half
    stacked = jnp.concatenate(
        [jnp.where(left_slot, queries, 0.0), jnp.where(left_slot, 0.0, queries)], axis=0
    ).astype(BF16)
    raw = dot_nt(stacked, need("keys")[...])
    tops, sums, weights = [], [], []
    for at in range(2):
        score = raw[at * n_blk : (at + 1) * n_blk, :] + shift[at]
        top = jnp.max(score, axis=1, keepdims=True)
        weight = jnp.exp(score - top)
        tops.append(top)
        sums.append(jnp.sum(weight, axis=1, keepdims=True))
        weights.append(weight.astype(BF16))
    summed = dot(jnp.concatenate(weights, axis=0), need("values")[...])
    summed = jnp.where(left_slot, summed[:n_blk, :], summed[n_blk:, :])
    column = iota((n_blk, width), 1)
    stats = jnp.where(
        column < 1,
        tops[0],
        jnp.where(column < 2, tops[1], jnp.where(column < 3, sums[0], sums[1])),
    )
    p_send[:, 0:1, :] = summed.reshape(n_blk, 1, width)
    p_send[:, 1:2, :] = stats.reshape(n_blk, 1, width)
    p_recv[pl.ds(me, 1)] = p_send[pl.ds(me, 1)]
    exchange_blk(p_send, p_recv, 1)
    wait_bytes(wo_all, chips - 1, recv_sem, 4)
    for far in (2, 1, 3):
        slot = (head + 2 * far) & (n_head - 1)
        share(wo_all.at[slot], slot, sibling, 5)
    wait_bytes(p_recv, n_blk - 1, recv_sem, 1)

    part_sum = p_recv[:, 0:1, :].reshape(n_blk, width)
    part_stat = p_recv[:, 1:2, :].reshape(n_blk, width)
    choose = (iota((8, width), 0) == iota((8, width), 1)).astype(F32)
    by_lane = dot_nt(choose, part_stat, HIGH)
    merged, total = [], []
    own_weight = []
    for at in range(2):
        part_top = by_lane[at : at + 1, :]
        part_total = by_lane[2 + at : 3 + at, :]
        top = jnp.maximum(
            own[at], jnp.max(jnp.where(holds, part_top, FLOOR), axis=1, keepdims=True)
        )
        factor = jnp.where(holds, jnp.exp(part_top - top), 0.0)
        mine_weight = jnp.exp(own[at] - top)
        total.append(jnp.sum(factor * part_total, axis=1, keepdims=True) + mine_weight)
        own_weight.append(mine_weight)
        merged.append(row_dot(factor, part_sum))
    value_final = jnp.where(left, merged[0], merged[1]) + jnp.where(
        left, own_weight[0], own_weight[1]
    ) * value_new
    attended = (value_final / jnp.where(left, total[0], total[1])).astype(BF16)
    c_recv[pl.ds(head, 1)] = attended.reshape(1, reqs, width)
    exchange_head(lambda to: c_recv.at[head], c_recv, 2)
    wait_bytes(wo_all, chips, recv_sem, 5)
    need("wo")
    wait_bytes(c_recv, n_head - 1, recv_sem, 2)
    attended_all = jnp.concatenate([c_recv[at] for at in range(n_head)], axis=1)
    projected = dot(attended_all, wo_all[...].reshape(d_model, d_model))
    mixed = (inputs + projected).astype(BF16).astype(F32)
    for at in range(n_head):
        mixed_ref[at] = mixed[:, at * width : (at + 1) * width]
    inverse = lax.rsqrt(jnp.mean(mixed * mixed, axis=1, keepdims=True) + 1e-05)
    hidden_in = (mixed * inverse * need("ffn_gain")[...]).astype(BF16)
    gate = dot(hidden_in, need("wg")[...])
    upper_units = dot(hidden_in, need("wu")[...])
    hidden = (gate * jax.nn.sigmoid(gate) * upper_units).astype(BF16)
    down = dot(hidden, need("wd")[...]).astype(BF16)
    for at in range(n_head):
        e_send[at] = down[:, at * width : (at + 1) * width]
    e_recv[pl.ds(head, 1)] = e_send[pl.ds(head, 1)]
    exchange_head(lambda to: e_send.at[to], e_recv, 3)
    wait_bytes(e_recv, n_head - 1, recv_sem, 3)
    part = e_recv[0].astype(F32)
    for at in range(1, n_head):
        part = part + e_recv[at].astype(F32)
    out_ref[...] = (mixed_ref[head] + part).astype(BF16)
    for ref, count, at in sent:
        wait_bytes(ref, count, send_sem, at)


def body(
    tokens,
    norm_gain,
    w_query,
    w_key,
    w_value,
    w_out,
    ffn_gain,
    w_gate,
    w_up,
    w_down,
    keys,
    values,
    key_variate,
    query_variate,
    bias,
    lengths,
    order,
    live_blocks,
):
    n_blk = lax.axis_size("blk")
    n_head = lax.axis_size("head")
    reqs, d_model = tokens.shape
    width = d_model // n_head
    operands = dict(
        tok=tokens,
        norm_gain=norm_gain.reshape(1, -1),
        ffn_gain=ffn_gain.reshape(1, -1),
        order=order.reshape(-1, 128),
        lens=lengths.reshape(-1, 128),
        query_variate=query_variate.reshape(-1, 128),
        key_variate=key_variate.reshape(1, -1),
        live=live_blocks.reshape(1, -1),
        wq=w_query,
        wk=w_key,
        wv=w_value,
        keys=keys,
        values=values,
        wo=w_out,
        wg=w_gate,
        wu=w_up,
        wd=w_down,
    )
    loads = [operands[name] for name in LOADS]
    return pl.pallas_call(
        kernel,
        out_shape=jax.ShapeDtypeStruct((reqs, width), BF16),
        in_specs=[pl.BlockSpec(memory_space=pltpu.SMEM)]
        + [pl.BlockSpec(memory_space=pltpu.HBM)] * len(loads),
        out_specs=pl.BlockSpec(memory_space=pltpu.VMEM),
        scratch_shapes=[
            pltpu.VMEM((n_head,) * (name == "wo") + x.shape, x.dtype)
            for name, x in zip(LOADS, loads)
        ]
        + [
            pltpu.VMEM((n_blk, 1, width), F32),
            pltpu.VMEM((n_blk, 1, width), F32),
            pltpu.VMEM((n_blk, 2, width), F32),
            pltpu.VMEM((n_blk, 2, width), F32),
        ]
        + [pltpu.VMEM((n_head, reqs, width), BF16)] * 3
        + [pltpu.VMEM((n_head, reqs, width), F32)]
        + [
            pltpu.SemaphoreType.DMA((len(loads),)),
            pltpu.SemaphoreType.DMA((6,)),
            pltpu.SemaphoreType.DMA((6,)),
        ],
        compiler_params=pltpu.CompilerParams(
            collective_id=0, has_side_effects=True, vmem_limit_bytes=56 * 1024 * 1024
        ),
    )(bias, *loads)


def solution(mesh):
    placed = (
        P("blk", None),
        P(),
        P(None, "head"),
        P(None, "head"),
        P(None, "head"),
        P("head", None),
        P(),
        P(None, "head"),
        P(None, "head"),
        P("head", None),
        P("blk", "head"),
        P("blk", "head"),
        P("blk"),
        P(),
        P(None, "head"),
        P(),
        P(),
        P("blk"),
    )
    return jax.shard_map(
        body, mesh=mesh, in_specs=placed, out_specs=P("blk", "head"), check_vma=False
    )
```

```python
import jax
import jax.numpy as jnp
from jax import lax
from jax.experimental import pallas as pl
from jax.experimental.pallas import tpu as pltpu
from jax.sharding import PartitionSpec as P

F32 = jnp.float32
BF16 = jnp.bfloat16
HIGH = lax.Precision.HIGHEST
FLOOR = -1e30
SIDE = 8
EARLY = 6


def iota(shape, dim):
    return lax.broadcasted_iota(jnp.int32, shape, dim)


def dot(a, b):
    return jnp.dot(a, b, preferred_element_type=F32)


def dot_nt(a, b, precision=None):
    return lax.dot_general(
        a, b, (((1,), (1,)), ((), ())), preferred_element_type=F32, precision=precision
    )


def dot_tn(a, b, precision=None):
    return lax.dot_general(
        a, b, (((0,), (0,)), ((), ())), preferred_element_type=F32, precision=precision
    )


def row_dot(a, b):
    return jnp.dot(a, b, preferred_element_type=F32, precision=HIGH)


LOADS = (
    "order",
    "lens",
    "query_variate",
    "tok",
    "norm_gain",
    "wq",
    "wk",
    "wv",
    "key_variate",
    "live",
    "keys",
    "values",
    "wo",
    "ffn_gain",
    "wg",
    "wu",
    "wd",
)


def ring(k):
    return min(k, SIDE - k)


FAR_FIRST = sorted(
    ((dz, dy) for dz in range(SIDE) for dy in range(SIDE) if dz or dy),
    key=lambda step: -ring(step[0]) - ring(step[1]),
)


def each_blk(me, act):
    low = SIDE - 1
    for dz, dy in FAR_FIRST:
        act(((me + SIDE * dz) & (SIDE * low)) | ((me + dy) & low))


def each_head(head, n_head, act):
    for far in (2, 1, 3):
        to = (head + 2 * far) & (n_head - 1)
        act(to)
        act(to ^ 1)
    act(head ^ 1)


def kernel(*refs):
    n_loads = len(LOADS)
    bias_ref = refs[0]
    from_hbm = dict(zip(LOADS, refs[1 : 1 + n_loads]))
    out_ref = refs[1 + n_loads]
    at_vmem = dict(zip(LOADS, refs[2 + n_loads : 2 + 2 * n_loads]))
    (
        q_send,
        q_recv,
        p_send,
        p_recv,
        c_recv,
        e_send,
        e_recv,
        mixed_ref,
        load_sem,
        send_sem,
        recv_sem,
    ) = refs[2 + 2 * n_loads :]
    n_blk = q_send.shape[0]
    n_head = c_recv.shape[0]
    reqs, d_model = at_vmem["tok"].shape
    pool = at_vmem["keys"].shape[0]
    n_live = at_vmem["live"].shape[1]
    block = pool // n_live
    width = c_recv.shape[2]
    half = width // 2
    scale = 1.0 / (half**0.5)
    me = lax.axis_index("blk")
    head = lax.axis_index("head")

    wo_all = at_vmem["wo"]
    at_vmem["wo"] = wo_all.at[head]
    copies = {
        name: pltpu.make_async_copy(from_hbm[name], at_vmem[name], load_sem.at[at])
        for at, name in enumerate(LOADS)
    }
    loaded = set()
    sent = []

    def need(name):
        if name not in loaded:
            loaded.add(name)
            copies[name].wait()
        return at_vmem[name]

    barrier = pltpu.get_barrier_semaphore()

    for name in LOADS[:EARLY]:
        copies[name].start()
    each_blk(me, lambda to: pl.semaphore_signal(barrier, inc=1, device_id={"blk": to}))
    each_head(
        head, n_head, lambda to: pl.semaphore_signal(barrier, inc=1, device_id={"head": to})
    )

    order = need("order")[...]
    rows, lanes = order.shape
    home = order[0:1, :] >> 5
    local = order & (reqs - 1)
    lens = need("lens")[...]
    coarse = (lens >> 6).astype(F32)
    fine = ((lens & 63) + (need("query_variate")[...] << 6)).astype(F32)
    both = jnp.concatenate([coarse, fine], axis=1).astype(BF16)
    per_row = lanes // reqs
    pick = jnp.concatenate(
        [
            (home == iota((rows, lanes), 0) * per_row + part).astype(F32)
            for part in range(per_row)
        ],
        axis=1,
    ).astype(BF16)
    found = dot_tn(both, pick)
    found = 256.0 * found[:lanes, :] + found[lanes:, :]
    table = jnp.zeros((reqs, lanes), F32)
    for part in range(per_row):
        at_row, at_lane = part * reqs, part * lanes
        table = table + found[at_row : at_row + reqs, at_lane : at_lane + lanes]
    picked = [jnp.where(local == slot, table[slot : slot + 1, :], 0.0) for slot in range(reqs)]
    while len(picked) > 1:
        picked = [a + b for a, b in zip(picked[::2], picked[1::2])]
    ordered = picked[0].astype(jnp.int32)
    variate = ((ordered >> 6) & 3).astype(F32)
    coarse = (ordered >> 8).astype(F32)
    fine = (ordered & 63).astype(F32)
    length = 64.0 * coarse + fine
    upper = (iota((lanes, lanes), 0) <= iota((lanes, lanes), 1)).astype(F32).astype(BF16)
    prefix = dot(jnp.concatenate([coarse, fine], axis=0).astype(BF16), upper)
    below = (iota((rows, rows), 1) < iota((rows, rows), 0)).astype(F32).astype(BF16)
    above = dot(below, jnp.concatenate([coarse, fine], axis=1).astype(BF16))
    above = jnp.sum(64.0 * above[:, :lanes] + above[:, lanes:], axis=1, keepdims=True)
    ends = 64.0 * prefix[:rows, :] + prefix[rows:, :] + above
    starts = ends - length

    mine = jnp.where(home == me, local, -1)
    start_acc = jnp.zeros((reqs, lanes), F32)
    end_acc = jnp.zeros((reqs, lanes), F32)
    slot_id = iota((reqs, lanes), 0)
    for row in range(rows):
        hit = mine[row : row + 1, :] == slot_id
        start_acc = start_acc + jnp.where(hit, starts[row : row + 1, :], 0.0)
        end_acc = end_acc + jnp.where(hit, ends[row : row + 1, :], 0.0)
    start_req = jnp.sum(start_acc, axis=1, keepdims=True)
    end_req = jnp.sum(end_acc, axis=1, keepdims=True)
    first = (iota((reqs, n_blk), 1) * pool).astype(F32)
    holds = (end_req > first) & (start_req < first + pool)
    holds_f = holds.astype(F32)

    inputs = need("tok")[...].astype(F32)
    mean_square = jnp.mean(inputs * inputs, axis=1, keepdims=True)
    normed = (inputs * lax.rsqrt(mean_square + 1e-05) * need("norm_gain")[...]).astype(BF16)
    query = dot(normed, need("wq")[...]).astype(BF16)
    query_f = query.astype(F32)
    routed = dot_tn(holds_f.astype(BF16), query) * scale
    q_send[...] = routed.reshape(n_blk, 1, width)
    q_recv[pl.ds(me, 1)] = q_send[pl.ds(me, 1)]

    pl.semaphore_wait(barrier, n_blk + n_head - 2)

    def exchange_blk(send, recv, at):
        def start(to):
            pltpu.make_async_remote_copy(
                src_ref=send.at[to],
                dst_ref=recv.at[me],
                send_sem=send_sem.at[at],
                recv_sem=recv_sem.at[at],
                device_id={"blk": to},
            ).start()

        each_blk(me, start)
        sent.append((send, n_blk - 1, at))

    def exchange_head(send, recv, at):
        def start(to):
            pltpu.make_async_remote_copy(
                src_ref=send(to),
                dst_ref=recv.at[head],
                send_sem=send_sem.at[at],
                recv_sem=recv_sem.at[at],
                device_id={"head": to},
            ).start()

        each_head(head, n_head, start)
        sent.append((recv, n_head - 1, at))

    def share(src, slot, to, at):
        pltpu.make_async_remote_copy(
            src_ref=src,
            dst_ref=wo_all.at[slot],
            send_sem=send_sem.at[at],
            recv_sem=recv_sem.at[at],
            device_id={"head": to},
        ).start()

    def wait_bytes(ref, count, sem, at):
        part = ref.at[pl.ds(0, count)]
        pltpu.make_async_copy(part, part, sem.at[at]).wait()

    exchange_blk(q_send, q_recv, 0)

    for name in LOADS[EARLY:]:
        copies[name].start()

    chips = n_head // 2
    sibling = head ^ 1
    for far in (2, 1, 3):
        share(from_hbm["wo"], head, (head + 2 * far) & (n_head - 1), 4)
    share(from_hbm["wo"], head, sibling, 5)
    sent.append((wo_all, chips - 1, 4))
    sent.append((wo_all, chips, 5))

    key_new = dot(normed, need("wk")[...]).astype(BF16).astype(F32)
    value_new = dot(normed, need("wv")[...]).astype(BF16).astype(F32)
    product = query_f * key_new
    left = iota((reqs, width), 1) < half
    own = [
        jnp.sum(jnp.where(left, product, 0.0), axis=1, keepdims=True) * scale + bias_ref[0, 0],
        jnp.sum(jnp.where(left, 0.0, product), axis=1, keepdims=True) * scale + bias_ref[0, 1],
    ]
    base = (me * pool).astype(F32)
    meets = (ends > base) & (starts < base + pool)
    start_lane = jnp.sum(jnp.where(meets, starts - base, 0.0), axis=0, keepdims=True)
    end_lane = jnp.sum(jnp.where(meets, ends - base, 0.0), axis=0, keepdims=True)
    variate_lane = jnp.sum(jnp.where(meets, variate, 0.0), axis=0, keepdims=True)
    at_home = home == iota((n_blk, lanes), 0)
    start_slot = jnp.sum(jnp.where(at_home, start_lane, 0.0), axis=1, keepdims=True)
    end_slot = jnp.sum(jnp.where(at_home, end_lane, 0.0), axis=1, keepdims=True)
    variate_slot = jnp.sum(jnp.where(at_home, variate_lane, 0.0), axis=1, keepdims=True)
    in_block = (iota((n_live, pool), 1) // block == iota((n_live, pool), 0)).astype(BF16)
    live = dot(jnp.broadcast_to(need("live")[...].astype(F32).astype(BF16), (8, n_live)), in_block)[0:1, :]
    token = iota((n_blk, pool), 1).astype(F32)
    mask = (token >= start_slot) & (token < end_slot) & (live > 0.5)
    same = need("key_variate")[...].astype(F32) == variate_slot

    shift = [
        jnp.where(mask, jnp.where(same, bias_ref[0, at], bias_ref[1, at]), FLOOR)
        for at in range(2)
    ]
    wait_bytes(q_recv, n_blk - 1, recv_sem, 0)
    queries = q_recv[...].reshape(n_blk, width)
    left_slot = iota((n_blk, width), 1) < half
    stacked = jnp.concatenate(
        [jnp.where(left_slot, queries, 0.0), jnp.where(left_slot, 0.0, queries)], axis=0
    ).astype(BF16)
    raw = dot_nt(stacked, need("keys")[...])
    tops, sums, weights = [], [], []
    for at in range(2):
        score = raw[at * n_blk : (at + 1) * n_blk, :] + shift[at]
        top = jnp.max(score, axis=1, keepdims=True)
        weight = jnp.exp(score - top)
        tops.append(top)
        sums.append(jnp.sum(weight, axis=1, keepdims=True))
        weights.append(weight.astype(BF16))
    summed = dot(jnp.concatenate(weights, axis=0), need("values")[...])
    summed = jnp.where(left_slot, summed[:n_blk, :], summed[n_blk:, :])
    column = iota((n_blk, width), 1)
    stats = jnp.where(
        column < 1,
        tops[0],
        jnp.where(column < 2, tops[1], jnp.where(column < 3, sums[0], sums[1])),
    )
    p_send[:, 0:1, :] = summed.reshape(n_blk, 1, width)
    p_send[:, 1:2, :] = stats.reshape(n_blk, 1, width)
    p_recv[pl.ds(me, 1)] = p_send[pl.ds(me, 1)]
    exchange_blk(p_send, p_recv, 1)
    wait_bytes(wo_all, chips - 1, recv_sem, 4)
    for far in (2, 1, 3):
        slot = (head + 2 * far) & (n_head - 1)
        share(wo_all.at[slot], slot, sibling, 5)
    wait_bytes(p_recv, n_blk - 1, recv_sem, 1)

    part_sum = p_recv[:, 0:1, :].reshape(n_blk, width)
    part_stat = p_recv[:, 1:2, :].reshape(n_blk, width)
    choose = (iota((8, width), 0) == iota((8, width), 1)).astype(F32)
    by_lane = dot_nt(choose, part_stat, HIGH)
    factors, total = [], []
    own_weight = []
    for at in range(2):
        part_top = by_lane[at : at + 1, :]
        part_total = by_lane[2 + at : 3 + at, :]
        top = jnp.maximum(
            own[at], jnp.max(jnp.where(holds, part_top, FLOOR), axis=1, keepdims=True)
        )
        factor = jnp.where(holds, jnp.exp(part_top - top), 0.0)
        mine_weight = jnp.exp(own[at] - top)
        total.append(jnp.sum(factor * part_total, axis=1, keepdims=True) + mine_weight)
        own_weight.append(mine_weight)
        factors.append(factor)
    factor = jnp.concatenate(factors, axis=0)
    factor_high = factor.astype(BF16)
    factor_low = (factor - factor_high.astype(F32)).astype(BF16)
    sum_high = part_sum.astype(BF16)
    sum_low = (part_sum - sum_high.astype(F32)).astype(BF16)
    merged = dot(
        jnp.concatenate([factor_high, factor_low], axis=1),
        jnp.concatenate([sum_high, sum_high], axis=0),
    ) + dot(factor_high, sum_low)
    value_final = jnp.where(left, merged[:reqs, :], merged[reqs:, :]) + jnp.where(
        left, own_weight[0], own_weight[1]
    ) * value_new
    attended = (value_final / jnp.where(left, total[0], total[1])).astype(BF16)
    c_recv[pl.ds(head, 1)] = attended.reshape(1, reqs, width)
    exchange_head(lambda to: c_recv.at[head], c_recv, 2)
    wait_bytes(wo_all, chips, recv_sem, 5)
    need("wo")
    wait_bytes(c_recv, n_head - 1, recv_sem, 2)
    attended_all = jnp.concatenate([c_recv[at] for at in range(n_head)], axis=1)
    projected = dot(attended_all, wo_all[...].reshape(d_model, d_model))
    mixed = (inputs + projected).astype(BF16).astype(F32)
    for at in range(n_head):
        mixed_ref[at] = mixed[:, at * width : (at + 1) * width]
    inverse = lax.rsqrt(jnp.mean(mixed * mixed, axis=1, keepdims=True) + 1e-05)
    hidden_in = (mixed * inverse * need("ffn_gain")[...]).astype(BF16)
    gate = dot(hidden_in, need("wg")[...])
    upper_units = dot(hidden_in, need("wu")[...])
    hidden = (gate * jax.nn.sigmoid(gate) * upper_units).astype(BF16)
    down = dot(hidden, need("wd")[...]).astype(BF16)
    for at in range(n_head):
        e_send[at] = down[:, at * width : (at + 1) * width]
    e_recv[pl.ds(head, 1)] = e_send[pl.ds(head, 1)]
    exchange_head(lambda to: e_send.at[to], e_recv, 3)
    wait_bytes(e_recv, n_head - 1, recv_sem, 3)
    part = e_recv[0].astype(F32)
    for at in range(1, n_head):
        part = part + e_recv[at].astype(F32)
    out_ref[...] = (mixed_ref[head] + part).astype(BF16)
    for ref, count, at in sent:
        wait_bytes(ref, count, send_sem, at)


def body(
    tokens,
    norm_gain,
    w_query,
    w_key,
    w_value,
    w_out,
    ffn_gain,
    w_gate,
    w_up,
    w_down,
    keys,
    values,
    key_variate,
    query_variate,
    bias,
    lengths,
    order,
    live_blocks,
):
    n_blk = lax.axis_size("blk")
    n_head = lax.axis_size("head")
    reqs, d_model = tokens.shape
    width = d_model // n_head
    operands = dict(
        tok=tokens,
        norm_gain=norm_gain.reshape(1, -1),
        ffn_gain=ffn_gain.reshape(1, -1),
        order=order.reshape(-1, 128),
        lens=lengths.reshape(-1, 128),
        query_variate=query_variate.reshape(-1, 128),
        key_variate=key_variate.reshape(1, -1),
        live=live_blocks.reshape(1, -1),
        wq=w_query,
        wk=w_key,
        wv=w_value,
        keys=keys,
        values=values,
        wo=w_out,
        wg=w_gate,
        wu=w_up,
        wd=w_down,
    )
    loads = [operands[name] for name in LOADS]
    return pl.pallas_call(
        kernel,
        out_shape=jax.ShapeDtypeStruct((reqs, width), BF16),
        in_specs=[pl.BlockSpec(memory_space=pltpu.SMEM)]
        + [pl.BlockSpec(memory_space=pltpu.HBM)] * len(loads),
        out_specs=pl.BlockSpec(memory_space=pltpu.VMEM),
        scratch_shapes=[
            pltpu.VMEM((n_head,) * (name == "wo") + x.shape, x.dtype)
            for name, x in zip(LOADS, loads)
        ]
        + [
            pltpu.VMEM((n_blk, 1, width), F32),
            pltpu.VMEM((n_blk, 1, width), F32),
            pltpu.VMEM((n_blk, 2, width), F32),
            pltpu.VMEM((n_blk, 2, width), F32),
        ]
        + [pltpu.VMEM((n_head, reqs, width), BF16)] * 3
        + [pltpu.VMEM((n_head, reqs, width), F32)]
        + [
            pltpu.SemaphoreType.DMA((len(loads),)),
            pltpu.SemaphoreType.DMA((6,)),
            pltpu.SemaphoreType.DMA((6,)),
        ],
        compiler_params=pltpu.CompilerParams(
            collective_id=0, has_side_effects=True, vmem_limit_bytes=56 * 1024 * 1024
        ),
    )(bias, *loads)


def solution(mesh):
    placed = (
        P("blk", None),
        P(),
        P(None, "head"),
        P(None, "head"),
        P(None, "head"),
        P("head", None),
        P(),
        P(None, "head"),
        P(None, "head"),
        P("head", None),
        P("blk", "head"),
        P("blk", "head"),
        P("blk"),
        P(),
        P(None, "head"),
        P(),
        P(),
        P("blk"),
    )
    return jax.shard_map(
        body, mesh=mesh, in_specs=placed, out_specs=P("blk", "head"), check_vma=False
    )
```
